32 devices in a mesh: region: 4 (over y, x), block: 8 (over z, core).
Axes of the slice: x: 2, y: 2, z: 4, core: 2. Of those that a mesh axis runs over, the one named last changes fastest.
Arguments:
- obs: bfloat16 [512, 32, 128], P(('region', 'block')), may hold values from -6 to 6
- predict: bfloat16 [512, 2, 128, 128], P(('region', 'block')), may hold values from -0.375 to 0.375
- factor: bfloat16 [512, 128, 128], P(('region', 'block')), as said below
- tau: float32 [32], replicated, may hold values from 0.5 to 2
- nbr_dev: int32 [512, 1], P(('region', 'block')), may hold values from 0 to 7; in each aligned block of 16 rows (0 to 15, 16 to 31, ...) at most 4 rows name the same one
- nbr_slot: int32 [512, 2], P(('region', 'block')), may hold values from 0 to 15
- counts: int32 [32], P(('region', 'block')), may hold values from 8 to 16
Outputs:
- grad_obs: float32 [512, 32, 128], P(('region', 'block'))
- grad_tau: float32 [32], replicated
The draws below stay inside these ranges and needn't reach their ends.
Inputs may be any that keep to these rules, and one draw needn't show every extreme that they name: `nbr_dev`: among the blocks of one device at most 4 name the same device. `nbr_slot`: column 0 is a slot on the in-region neighbour's device, column 1 a slot on the device of the previous region with the same index along block. `factor`: each block's matrix is the identity plus small entries.
All inputs are finite; a program needn't handle non-finite values.
Results may differ from the reference program's by a relative error of at most 0.0035.
Values may be sent and summed in bfloat16 or wider, within the bound.
A program may use at most 64 MiB of HBM per device.

```python
import math
import jax
import jax.numpy as jnp
import numpy as np
from jax import lax

C = 32
BS = 128
NBD = 16
CAP = 4
NB = 512
N_REGION = 4
N_BLOCK = 8


def draw_factor(key, part):
    first_key = jax.random.fold_in(key, 0)
    off = jax.random.normal(first_key, (NB, BS, BS), jnp.float32)
    scaled = off * (0.5 / BS ** 0.5)
    return (scaled + jnp.eye(BS, dtype=jnp.float32)[None]).astype(jnp.bfloat16)


def touch_ends(values, stream_key, low, largest):
    longest = values.shape.index(max(values.shape))
    spots = []
    for shift in (0, 1):
        where = [jax.random.randint(jax.random.fold_in(stream_key, axis), (), 0, length) for axis, length in enumerate(values.shape)]
        where[longest] = (where[longest] + shift) % values.shape[longest]
        spots.append(tuple(where))
    return values.at[spots[0]].set(low).at[spots[1]].set(largest)


def levels(rng, dims, shards, smallest, top_value):
    def one(dim, blocks):
        steps = jax.random.uniform(jax.random.fold_in(jax.random.fold_in(rng, 6), dim), (blocks,), jnp.float32, smallest / len(shards), top_value / len(shards))
        return jnp.repeat(jnp.exp(steps), dims[dim] // blocks).reshape((-1,) + (1,) * (len(dims) - dim - 1))

    level = one(*shards[0])
    for cut in shards[1:]:
        level = level * one(*cut)
    return level


def shared_out(key, own, number, rows, amount, top, most, lean):
    sequence = jax.random.permutation(key, amount)
    packed, common = portions_of(amount, rows * top, most, lean, True), portions_of(amount, rows * top, most, lean, False)
    places = jnp.arange(amount)

    def named(sizes, turn):
        used = int((sizes > 0).sum())
        fixed = max(1, used // 4)
        moved = fixed + (places - fixed + turn * (used - fixed)) % max(1, amount - fixed)
        return jnp.zeros((amount,), jnp.int32).at[sequence[jnp.where(places < fixed, places, moved)]].set(jnp.asarray(sizes, jnp.int32))

    sizes = jnp.where(number % 4 == 0, named(packed, number // 4), named(common, number - number // 4 - 1))
    mixed = jax.random.permutation(jax.random.fold_in(own, 3), amount)
    donor, sink = mixed[0:amount // 2 * 2:2], mixed[1:amount // 2 * 2:2]
    margin = jnp.minimum(sizes[donor] - 1, most - sizes[sink]) // 2
    margin = jnp.where((donor == sequence[0]) | (sink == sequence[0]) | (sizes[sink] == 0), 0, jnp.maximum(margin, 0))
    moved = jax.random.randint(jax.random.fold_in(own, 4), (amount // 2,), 0, 1 << 20) % (margin + 1)
    sizes = sizes.at[donor].add(-moved).at[sink].add(moved)
    items = jnp.searchsorted(jnp.cumsum(sizes), jnp.arange(rows * top), side="right").astype(jnp.int32)
    listing = items.reshape(top, rows).T
    listing = listing[jax.random.permutation(jax.random.fold_in(own, 1), rows)]
    turn = jax.random.randint(jax.random.fold_in(own, 2), (rows, 1), 0, top)
    return jnp.take_along_axis(listing, (jnp.arange(top)[None, :] + turn) % top, axis=1)


def portions_of(count, total, reach, slope, full):
    loads = [(1 << 20) // math.isqrt(grade ** slope) + 1 for grade in range(1, count + 1)]
    largest = reach if full else min(reach, max(-(-total // count), total * loads[0] // sum(loads)))
    least = 1 if total - largest >= count - 1 else 0
    holding, spare = [largest] + [least] * (count - 1), total - largest - least * (count - 1)
    while spare > 0:
        free = [i for i in range(1, count) if holding[i] < largest] or [i for i in range(1, count) if holding[i] < reach]
        whole, left = sum([loads[i] for i in free]), spare
        for i in free:
            addition = min(reach - holding[i], max(1, left * loads[i] // whole), spare)
            holding[i] = holding[i] + addition
            spare = spare - addition
    return np.array(holding)


def noise(rng, extent, width, reach, shards=(), kind=jnp.bfloat16):
    drawn = jax.random.normal(rng, extent, jnp.float32) * width
    if len(shards) > 0:
        drawn = levels(rng, extent, shards, -0.22, 0.18) * drawn
    return jnp.clip(drawn, min=-reach, max=reach).astype(kind)


def setup_inputs(seed: int = 0) -> dict:
    seeds = jax.random.split(jax.random.key(seed), 8)
    obs = noise(seeds[0], (NB, C, BS), 1.0, 6.0, ((0, 32),))
    predict = noise(seeds[1], (NB, 2, BS, BS), (2 * BS) ** -0.5, 0.375, ((0, 32),))
    factor = draw_factor(jax.random.fold_in(seeds[7], 71), 0)
    tau = jnp.clip(jnp.exp(jax.random.uniform(seeds[3], (C,), jnp.float32, math.log(0.5), math.log(2.0))), 0.5, 2.0)
    nbr_dev_keys = jax.random.split(jax.random.fold_in(seeds[4], 1), NB // NBD)
    nbr_dev_turns = jax.random.permutation(jax.random.fold_in(seeds[4], 3), NB // NBD)
    nbr_dev = jax.vmap(lambda own, number: shared_out(jax.random.fold_in(seeds[4], 2), own, number, NBD, N_BLOCK, 1, CAP, 1))(nbr_dev_keys, nbr_dev_turns).reshape((NB, 1))
    nbr_slot = touch_ends(jax.random.randint(seeds[5], (NB, 2), 0, NBD), jax.random.fold_in(seeds[5], 1), 0, NBD - 1).astype(jnp.int32)
    counts = touch_ends(jax.random.randint(seeds[6], (N_REGION * N_BLOCK,), NBD // 2, NBD + 1), jax.random.fold_in(seeds[6], 1), NBD // 2, NBD).astype(jnp.int32)
    return {"obs": obs, "predict": predict, "factor": factor, "tau": tau, "nbr_dev": nbr_dev, "nbr_slot": nbr_slot, "counts": counts}


def reference(obs, predict, factor, tau, nbr_dev, nbr_slot, counts):
    nb = obs.shape[0]
    groups = nb // NBD
    index = jnp.arange(nb, dtype=jnp.int32)
    dev_of = index // NBD
    region = dev_of // N_BLOCK
    inner = dev_of % N_BLOCK
    slot = index % NBD
    first = (region * N_BLOCK + nbr_dev[:, 0]) * NBD + nbr_slot[:, 0]
    seam = region > 0
    second = jnp.where(seam, ((region - 1) * N_BLOCK + inner) * NBD + nbr_slot[:, 1], 0).astype(jnp.int32)
    live = (slot < counts[dev_of]).astype(jnp.float32)
    seam_f = seam.astype(jnp.float32)
    near = jnp.take(obs, first, axis=0)
    far = jnp.take(obs, second, axis=0)

    def shape_g(a):
        return a.reshape((groups, NBD) + a.shape[1:])

    def per_device(items):
        own, pred, fac, y_one, y_two, seam_g, live_g = items
        p_zero = pred[:, 0].astype(jnp.float32)
        p_one = pred[:, 1].astype(jnp.float32)
        err = own.astype(jnp.float32) - jnp.einsum('bcj,bjk->bck', y_one.astype(jnp.float32), p_zero)
        err = err - seam_g[:, None, None] * jnp.einsum('bcj,bjk->bck', y_two.astype(jnp.float32), p_one)
        err = err.astype(jnp.bfloat16)
        facf = fac.astype(jnp.float32)
        white = jnp.einsum('bcj,bjk->bck', err.astype(jnp.float32), facf)
        weighted = (live_g[:, None, None] * tau[None, :, None] * white).astype(jnp.bfloat16)
        adj = jnp.einsum('bck,bjk->bcj', weighted.astype(jnp.float32), facf)
        adj16 = adj.astype(jnp.bfloat16).astype(jnp.float32)
        back_one = -jnp.einsum('bck,bjk->bcj', adj16, p_zero)
        back_two = -seam_g[:, None, None] * jnp.einsum('bck,bjk->bcj', adj16, p_one)
        squares = jnp.sum(live_g[:, None, None] * white * white, axis=(0, 2))
        return adj, back_one, back_two, squares

    adj, back_one, back_two, squares = lax.map(per_device, (shape_g(obs), shape_g(predict), shape_g(factor), shape_g(near), shape_g(far), shape_g(seam_f), shape_g(live)))
    grad = adj.reshape(obs.shape)
    grad = grad.at[first].add(back_one.reshape(obs.shape))
    grad = grad.at[second].add(back_two.reshape(obs.shape))
    total_sq = jnp.sum(squares, axis=0)
    total_live = jnp.sum(live)
    grad_tau = (0.5 * total_sq - 0.5 * BS * total_live / tau) / (nb * BS)
    return grad, grad_tau
```

```python
import functools

import jax
import jax.numpy as jnp
from jax import lax
from jax.experimental import pallas as pl
from jax.experimental.pallas import tpu as pltpu
from jax.sharding import PartitionSpec as P

MESH = pl.DeviceIdType.MESH
LANES = 128


def kernel(
    nblock,
    nregion,
    cap,
    dev_ref,
    slot_ref,
    counts_ref,
    tau_ref,
    obs_hbm,
    predict_hbm,
    factor_hbm,
    out_ref,
    gtau_ref,
    obs,
    predict,
    factor,
    req_send,
    req_recv,
    near_send,
    near_recv,
    ret_send,
    ret_recv,
    seam_obs,
    seam_tgt,
    seam_tgt_in,
    seam_ret,
    seam_ret_in,
    place,
    spread,
    partial,
    back,
    adjoint,
    sq_send,
    sq_recv,
    rg_send,
    rg_recv,
    local_sem,
    req_ss,
    req_rs,
    near_ss,
    near_rs,
    ret_ss,
    ret_rs,
    sq_ss,
    sq_rs,
    rg_ss,
    rg_rs,
    seam_ss,
    seam_rs,
):
    nbd, chans, width = obs.shape
    rows = nbd * chans
    part = cap * chans
    lanes = req_send.shape[2]
    me = lax.axis_index("block")
    region = lax.axis_index("region")
    bf16, f32, i32 = jnp.bfloat16, jnp.float32, jnp.int32

    def each_peer(body):
        if nblock <= 8:
            for step in range(1, nblock):
                body(lax.rem(me + step, nblock))
        else:

            def run(step, carry):
                body(lax.rem(me + step, nblock))
                return carry

            lax.fori_loop(1, nblock, run, 0)

    def each_region(body):
        for step in range(1, nregion):
            body(lax.rem(region + step, nregion))

    def to_block(src, dst, ss, rs, peer):
        return pltpu.make_async_remote_copy(
            src_ref=src,
            dst_ref=dst,
            send_sem=ss,
            recv_sem=rs,
            device_id={"block": peer},
            device_id_type=MESH,
        )

    def to_region(src, dst, ss, rs, peer):
        return pltpu.make_async_remote_copy(
            src_ref=src,
            dst_ref=dst,
            send_sem=ss,
            recv_sem=rs,
            device_id={"region": peer},
            device_id_type=MESH,
        )

    barrier = pltpu.get_barrier_semaphore()
    each_peer(
        lambda peer: pl.semaphore_signal(
            barrier, inc=1, device_id={"block": peer}, device_id_type=MESH
        )
    )
    each_region(
        lambda peer: pl.semaphore_signal(
            barrier, inc=1, device_id={"region": peer}, device_id_type=MESH
        )
    )
    load_obs = pltpu.make_async_copy(obs_hbm, obs, local_sem.at[0])
    load_predict = pltpu.make_async_copy(predict_hbm, predict, local_sem.at[1])
    load_factor = pltpu.make_async_copy(factor_hbm, factor, local_sem.at[2])
    load_obs.start()
    load_predict.start()
    load_factor.start()

    dest = [dev_ref[h, 0] for h in range(nbd)]
    flat = []
    for h in range(nbd):
        rank = jnp.int32(0)
        for g in range(h):
            rank = rank + (dest[g] == dest[h]).astype(i32)
        flat.append(dest[h] * cap + rank)

    lane = lax.broadcasted_iota(i32, (nblock, lanes), 1)
    spot = lax.broadcasted_iota(i32, (nblock, lanes), 0) * cap + lane // chans
    spot = jnp.where(lane < part, spot, -1)
    wanted = jnp.full((nblock, lanes), -1, i32)
    for h in range(nbd):
        wanted = jnp.where(spot == flat[h], slot_ref[h, 0] * chans + lane % chans, wanted)
    for d in range(nblock):
        req_send[d] = wanted[d : d + 1]

    block_lane = lax.broadcasted_iota(i32, (1, rows), 1)
    owner_of = block_lane // chans
    flat_row = jnp.zeros((1, rows), i32)
    seam_row = jnp.zeros((1, rows), i32)
    for h in range(nbd):
        flat_row = jnp.where(owner_of == h, flat[h], flat_row)
        seam_row = jnp.where(owner_of == h, slot_ref[h, 1], seam_row)
    flat_row = flat_row * chans + block_lane % chans
    seam_tgt[...] = seam_row * chans + block_lane % chans

    pl.semaphore_wait(barrier, nblock - 1 + nregion - 1)

    def request(peer, mine):
        return to_block(req_send.at[peer], req_recv.at[mine], req_ss.at[peer], req_rs.at[mine], peer)

    each_peer(lambda peer: request(peer, me).start())
    req_recv[me] = req_send[me]

    down = lax.rem(region + 1, nregion)
    up = lax.rem(region + nregion - 1, nregion)
    seam_fwd = to_region(obs_hbm, seam_obs, seam_ss.at[0], seam_rs.at[0], down)
    seam_where = to_region(seam_tgt, seam_tgt_in, seam_ss.at[1], seam_rs.at[1], up)
    seam_bwd = to_region(seam_ret, seam_ret_in, seam_ss.at[2], seam_rs.at[2], up)
    has_prev = region > 0
    has_next = region < nregion - 1

    @pl.when(has_next)
    def _():
        seam_fwd.start()

    @pl.when(has_prev)
    def _():
        seam_where.start()

    load_obs.wait()
    pick_lane = lax.broadcasted_iota(i32, (part, rows), 1)

    def picked(peer):
        row = jnp.broadcast_to(req_recv[peer], (LANES, lanes))
        column = jnp.transpose(row)[:part]
        column = jnp.concatenate([column] * (rows // LANES), axis=1)
        mask = jnp.where(column == pick_lane, 1.0, 0.0).astype(bf16)
        got = jnp.dot(mask, obs[...].reshape(rows, width), preferred_element_type=f32)
        return got.astype(bf16).reshape(cap, chans, width)

    def span(d):
        return pl.ds(d * cap, cap)

    def serve(peer, mine):
        return to_block(
            near_send.at[span(peer)],
            near_recv.at[span(mine)],
            near_ss.at[peer],
            near_rs.at[mine],
            peer,
        )

    def answer(peer):
        request(me, peer).wait_recv()
        near_send[span(peer)] = picked(peer)
        serve(peer, me).start()

    each_peer(answer)
    near_recv[span(me)] = picked(me)

    place_row = lax.broadcasted_iota(i32, (part, rows), 0)

    def build(d):
        place[d] = jnp.where(flat_row - d * part == place_row, 1.0, 0.0).astype(bf16)
        spread[d] = jnp.where(
            req_recv[d][:, :part] == lax.broadcasted_iota(i32, (rows, part), 0), 1.0, 0.0
        ).astype(bf16)

    each_peer(build)
    build(me)

    @pl.when(has_prev)
    def _():
        seam_fwd.wait_recv()

    @pl.when(jnp.logical_not(has_prev))
    def _():
        seam_obs[...] = jnp.zeros_like(seam_obs)

    load_predict.wait()
    for g in range(nbd):
        partial[g] = obs[g].astype(f32) - jnp.dot(
            seam_obs[slot_ref[g, 1]], predict[g, 1], preferred_element_type=f32
        )
    load_factor.wait()

    eye = lax.broadcasted_iota(i32, (chans, LANES), 0) == lax.broadcasted_iota(
        i32, (chans, LANES), 1
    )
    tau_row = jnp.concatenate([tau_ref[...], jnp.zeros((1, LANES - chans), f32)], axis=1)
    tau_col = jnp.sum(jnp.where(eye, tau_row, 0.0), axis=1, keepdims=True)
    count = counts_ref[0]

    each_peer(lambda peer: serve(me, peer).wait_recv())

    squares = jnp.zeros((chans, width), f32)
    nt = (((1,), (1,)), ((), ()))
    for g in range(nbd):
        err = partial[g] - jnp.dot(near_recv[flat[g]], predict[g, 0], preferred_element_type=f32)
        white = jnp.dot(err.astype(bf16), factor[g], preferred_element_type=f32)
        live = (g < count).astype(f32)
        squares = squares + live * white * white
        weighted = (live * tau_col * white).astype(bf16)
        adj = lax.dot_general(weighted, factor[g], nt, preferred_element_type=f32)
        out_ref[g] = adj
        adj16 = adj.astype(bf16)
        adjoint[g] = adj16
        back[g] = lax.dot_general(adj16, predict[g, 0], nt, preferred_element_type=f32).astype(bf16)

    def placed(peer):
        got = jnp.dot(place[peer], back[...].reshape(rows, width), preferred_element_type=f32)
        return got.astype(bf16)

    def give(peer, mine):
        return to_block(ret_send.at[peer], ret_recv.at[mine], ret_ss.at[peer], ret_rs.at[mine], peer)

    def give_back(peer):
        ret_send[peer] = placed(peer)
        give(peer, me).start()

    each_peer(give_back)
    ret_recv[me] = placed(me)

    @pl.when(has_prev)
    def _():
        for g in range(nbd):
            seam_ret[g] = lax.dot_general(
                adjoint[g], predict[g, 1], nt, preferred_element_type=f32
            ).astype(bf16)
        seam_bwd.start()

    live_lane = lax.broadcasted_iota(i32, (1, LANES), 1) == chans
    sums = jnp.sum(
        jnp.where(eye, jnp.sum(squares, axis=1, keepdims=True), 0.0), axis=0, keepdims=True
    )
    sums = sums + jnp.where(live_lane, jnp.minimum(count, nbd).astype(f32), 0.0)
    sq_send[...] = sums

    def share(peer, mine):
        return to_block(sq_send, sq_recv.at[mine], sq_ss.at[peer], sq_rs.at[mine], peer)

    each_peer(lambda peer: share(peer, me).start())
    sq_recv[me] = sums
    each_peer(lambda peer: share(me, peer).wait_recv())
    line = sq_recv[0]
    for d in range(1, nblock):
        line = line + sq_recv[d]
    rg_send[...] = line

    def share_region(peer, mine):
        return to_region(rg_send, rg_recv.at[mine], rg_ss.at[peer], rg_rs.at[mine], peer)

    each_region(lambda peer: share_region(peer, region).start())
    rg_recv[region] = line

    @pl.when(has_next)
    def _():
        seam_where_in = to_region(seam_tgt, seam_tgt_in, seam_ss.at[1], seam_rs.at[1], up)
        seam_where_in.wait_recv()
        mask = jnp.where(
            seam_tgt_in[...] == lax.broadcasted_iota(i32, (rows, rows), 0), 1.0, 0.0
        ).astype(bf16)
        seam_bwd.wait_recv()
        got = jnp.dot(mask, seam_ret_in[...].reshape(rows, width), preferred_element_type=f32)
        out_ref[...] = out_ref[...] - got.reshape(nbd, chans, width)

    def add(d):
        got = jnp.dot(spread[d], ret_recv[d], preferred_element_type=f32)
        out_ref[...] = out_ref[...] - got.reshape(nbd, chans, width)

    add(me)

    each_region(lambda peer: share_region(region, peer).wait_recv())
    total = rg_recv[0]
    for r in range(1, nregion):
        total = total + rg_recv[r]
    total_live = jnp.sum(jnp.where(live_lane, total, 0.0), axis=1, keepdims=True)
    blocks = nbd * nblock * nregion
    gtau_ref[...] = (
        0.5 * total[:, :chans] - 0.5 * width * total_live / tau_ref[...]
    ) / (blocks * width)

    def take(peer):
        give(me, peer).wait_recv()
        add(peer)

    each_peer(take)

    def sent(peer):
        request(peer, me).wait_send()
        serve(peer, me).wait_send()
        give(peer, me).wait_send()
        share(peer, me).wait_send()

    each_peer(sent)
    each_region(lambda peer: share_region(peer, region).wait_send())

    @pl.when(has_next)
    def _():
        seam_fwd.wait_send()

    @pl.when(has_prev)
    def _():
        seam_where.wait_send()
        seam_bwd.wait_send()


def shards(obs, predict, factor, tau, nbr_dev, nbr_slot, counts):
    nbd, chans, width = obs.shape
    nblock = lax.axis_size("block")
    nregion = lax.axis_size("region")
    cap = max(2, 2 * nbd // nblock)
    rows = nbd * chans
    part = cap * chans
    lanes = -(-part // LANES) * LANES
    bf16, f32, i32 = jnp.bfloat16, jnp.float32, jnp.int32
    smem = pl.BlockSpec(memory_space=pltpu.SMEM)
    vmem = pl.BlockSpec(memory_space=pltpu.VMEM)
    hbm = pl.BlockSpec(memory_space=pl.ANY)
    dma = pltpu.SemaphoreType.DMA
    grad_obs, grad_tau = pl.pallas_call(
        functools.partial(kernel, nblock, nregion, cap),
        out_shape=(
            jax.ShapeDtypeStruct((nbd, chans, width), f32),
            jax.ShapeDtypeStruct((1, chans), f32),
        ),
        in_specs=[smem, smem, smem, vmem, hbm, hbm, hbm],
        out_specs=(vmem, vmem),
        scratch_shapes=[
            pltpu.VMEM((nbd, chans, width), bf16),
            pltpu.VMEM((nbd, 2, width, width), bf16),
            pltpu.VMEM((nbd, width, width), bf16),
            pltpu.VMEM((nblock, 1, lanes), i32),
            pltpu.VMEM((nblock, 1, lanes), i32),
            pltpu.VMEM((nblock * cap, chans, width), bf16),
            pltpu.VMEM((nblock * cap, chans, width), bf16),
            pltpu.VMEM((nblock, part, width), bf16),
            pltpu.VMEM((nblock, part, width), bf16),
            pltpu.VMEM((nbd, chans, width), bf16),
            pltpu.VMEM((1, rows), i32),
            pltpu.VMEM((1, rows), i32),
            pltpu.VMEM((nbd, chans, width), bf16),
            pltpu.VMEM((nbd, chans, width), bf16),
            pltpu.VMEM((nblock, part, rows), bf16),
            pltpu.VMEM((nblock, rows, part), bf16),
            pltpu.VMEM((nbd, chans, width), f32),
            pltpu.VMEM((nbd, chans, width), bf16),
            pltpu.VMEM((nbd, chans, width), bf16),
            pltpu.VMEM((1, LANES), f32),
            pltpu.VMEM((nblock, 1, LANES), f32),
            pltpu.VMEM((1, LANES), f32),
            pltpu.VMEM((nregion, 1, LANES), f32),
            dma((3,)),
            dma((nblock,)),
            dma((nblock,)),
            dma((nblock,)),
            dma((nblock,)),
            dma((nblock,)),
            dma((nblock,)),
            dma((nblock,)),
            dma((nblock,)),
            dma((nregion,)),
            dma((nregion,)),
            dma((3,)),
            dma((3,)),
        ],
        compiler_params=pltpu.CompilerParams(
            collective_id=0, has_side_effects=True, vmem_limit_bytes=40 << 20
        ),
        name="vecchia",
    )(nbr_dev, nbr_slot, counts, tau.reshape(1, chans), obs, predict, factor)
    return grad_obs, grad_tau.reshape(chans)


def solution(mesh):
    in_specs = (
        P(("region", "block"), None, None),
        P(("region", "block"), None, None, None),
        P(("region", "block"), None, None),
        P(),
        P(("region", "block"), None),
        P(("region", "block"), None),
        P(("region", "block")),
    )
    out_specs = (P(("region", "block"), None, None), P())
    return jax.shard_map(shards, mesh=mesh, in_specs=in_specs, out_specs=out_specs, check_vma=False)
```

```python
import functools

import jax
import jax.numpy as jnp
from jax import lax
from jax.experimental import pallas as pl
from jax.experimental.pallas import tpu as pltpu
from jax.sharding import PartitionSpec as P

MESH = pl.DeviceIdType.MESH
LANES = 128


def kernel(
    nblock,
    nregion,
    cap,
    dev_hbm,
    slot_hbm,
    counts_hbm,
    tau_hbm,
    obs_hbm,
    predict_hbm,
    factor_hbm,
    out_ref,
    gtau_ref,
    dev_ref,
    slot_ref,
    counts_ref,
    tau_ref,
    obs,
    predict,
    factor,
    req_send,
    req_recv,
    near_send,
    near_recv,
    ret_send,
    ret_recv,
    seam_obs,
    seam_tgt,
    seam_tgt_in,
    seam_ret,
    seam_ret_in,
    place,
    spread,
    partial,
    back,
    adjoint,
    sq_send,
    sq_recv,
    rg_send,
    rg_recv,
    local_sem,
    req_ss,
    req_rs,
    near_ss,
    near_rs,
    ret_ss,
    ret_rs,
    sq_ss,
    sq_rs,
    rg_ss,
    rg_rs,
    seam_ss,
    seam_rs,
):
    nbd, chans, width = obs.shape
    rows = nbd * chans
    part = cap * chans
    lanes = req_send.shape[2]
    me = lax.axis_index("block")
    region = lax.axis_index("region")
    bf16, f32, i32 = jnp.bfloat16, jnp.float32, jnp.int32

    def each_peer(body):
        if nblock <= 8:
            for step in range(1, nblock):
                body(lax.rem(me + step, nblock))
        else:

            def run(step, carry):
                body(lax.rem(me + step, nblock))
                return carry

            lax.fori_loop(1, nblock, run, 0)

    def each_region(body):
        for step in range(1, nregion):
            body(lax.rem(region + step, nregion))

    def to_block(src, dst, ss, rs, peer):
        return pltpu.make_async_remote_copy(
            src_ref=src,
            dst_ref=dst,
            send_sem=ss,
            recv_sem=rs,
            device_id={"block": peer},
            device_id_type=MESH,
        )

    def to_region(src, dst, ss, rs, peer):
        return pltpu.make_async_remote_copy(
            src_ref=src,
            dst_ref=dst,
            send_sem=ss,
            recv_sem=rs,
            device_id={"region": peer},
            device_id_type=MESH,
        )

    small = [
        pltpu.make_async_copy(src, dst, local_sem.at[3 + i])
        for i, (src, dst) in enumerate(
            [(dev_hbm, dev_ref), (slot_hbm, slot_ref), (counts_hbm, counts_ref), (tau_hbm, tau_ref)]
        )
    ]
    for copy in small:
        copy.start()

    barrier = pltpu.get_barrier_semaphore()
    each_peer(
        lambda peer: pl.semaphore_signal(
            barrier, inc=1, device_id={"block": peer}, device_id_type=MESH
        )
    )
    each_region(
        lambda peer: pl.semaphore_signal(
            barrier, inc=1, device_id={"region": peer}, device_id_type=MESH
        )
    )
    load_obs = pltpu.make_async_copy(obs_hbm, obs, local_sem.at[0])
    load_predict = pltpu.make_async_copy(predict_hbm, predict, local_sem.at[1])
    load_factor = pltpu.make_async_copy(factor_hbm, factor, local_sem.at[2])
    load_obs.start()
    load_predict.start()
    load_factor.start()

    for copy in small:
        copy.wait()

    dest = [dev_ref[0, h] for h in range(nbd)]
    flat = []
    for h in range(nbd):
        rank = jnp.int32(0)
        for g in range(h):
            rank = rank + (dest[g] == dest[h]).astype(i32)
        flat.append(dest[h] * cap + rank)

    lane = lax.broadcasted_iota(i32, (nblock, lanes), 1)
    spot = lax.broadcasted_iota(i32, (nblock, lanes), 0) * cap + lane // chans
    spot = jnp.where(lane < part, spot, -1)
    wanted = jnp.full((nblock, lanes), -1, i32)
    for h in range(nbd):
        wanted = jnp.where(spot == flat[h], slot_ref[0, h] * chans + lane % chans, wanted)
    for d in range(nblock):
        req_send[d] = wanted[d : d + 1]

    block_lane = lax.broadcasted_iota(i32, (1, rows), 1)
    owner_of = block_lane // chans
    flat_row = jnp.zeros((1, rows), i32)
    seam_row = jnp.zeros((1, rows), i32)
    for h in range(nbd):
        flat_row = jnp.where(owner_of == h, flat[h], flat_row)
        seam_row = jnp.where(owner_of == h, slot_ref[1, h], seam_row)
    flat_row = flat_row * chans + block_lane % chans
    seam_tgt[...] = seam_row * chans + block_lane % chans

    pl.semaphore_wait(barrier, nblock - 1 + nregion - 1)

    def request(peer, mine):
        return to_block(req_send.at[peer], req_recv.at[mine], req_ss.at[peer], req_rs.at[mine], peer)

    each_peer(lambda peer: request(peer, me).start())
    req_recv[me] = req_send[me]

    down = lax.rem(region + 1, nregion)
    up = lax.rem(region + nregion - 1, nregion)
    seam_fwd = to_region(obs_hbm, seam_obs, seam_ss.at[0], seam_rs.at[0], down)
    seam_where = to_region(seam_tgt, seam_tgt_in, seam_ss.at[1], seam_rs.at[1], up)
    seam_bwd = to_region(seam_ret, seam_ret_in, seam_ss.at[2], seam_rs.at[2], up)
    has_prev = region > 0
    has_next = region < nregion - 1

    @pl.when(has_next)
    def _():
        seam_fwd.start()

    @pl.when(has_prev)
    def _():
        seam_where.start()

    load_obs.wait()
    pick_lane = lax.broadcasted_iota(i32, (part, rows), 1)

    def picked(peer):
        row = jnp.broadcast_to(req_recv[peer], (LANES, lanes))
        column = jnp.transpose(row)[:part]
        column = jnp.concatenate([column] * (rows // LANES), axis=1)
        mask = jnp.where(column == pick_lane, 1.0, 0.0).astype(bf16)
        got = jnp.dot(mask, obs[...].reshape(rows, width), preferred_element_type=f32)
        return got.astype(bf16).reshape(cap, chans, width)

    def span(d):
        return pl.ds(d * cap, cap)

    def serve(peer, mine):
        return to_block(
            near_send.at[span(peer)],
            near_recv.at[span(mine)],
            near_ss.at[peer],
            near_rs.at[mine],
            peer,
        )

    def answer(peer):
        request(me, peer).wait_recv()
        near_send[span(peer)] = picked(peer)
        serve(peer, me).start()

    each_peer(answer)
    near_recv[span(me)] = picked(me)

    place_row = lax.broadcasted_iota(i32, (part, rows), 0)

    def build(d):
        place[d] = jnp.where(flat_row - d * part == place_row, 1.0, 0.0).astype(bf16)
        spread[d] = jnp.where(
            req_recv[d][:, :part] == lax.broadcasted_iota(i32, (rows, part), 0), 1.0, 0.0
        ).astype(bf16)

    each_peer(build)
    build(me)

    @pl.when(has_prev)
    def _():
        seam_fwd.wait_recv()

    @pl.when(jnp.logical_not(has_prev))
    def _():
        seam_obs[...] = jnp.zeros_like(seam_obs)

    load_predict.wait()
    for g in range(nbd):
        partial[g] = obs[g].astype(f32) - jnp.dot(
            seam_obs[slot_ref[1, g]], predict[g, 1], preferred_element_type=f32
        )
    load_factor.wait()

    eye = lax.broadcasted_iota(i32, (chans, LANES), 0) == lax.broadcasted_iota(
        i32, (chans, LANES), 1
    )
    tau_row = jnp.concatenate([tau_ref[...], jnp.zeros((1, LANES - chans), f32)], axis=1)
    tau_col = jnp.sum(jnp.where(eye, tau_row, 0.0), axis=1, keepdims=True)
    count = counts_ref[0]

    each_peer(lambda peer: serve(me, peer).wait_recv())

    nt = (((1,), (1,)), ((), ()))
    every = range(nbd)
    err = [
        (
            partial[g]
            - jnp.dot(near_recv[flat[g]], predict[g, 0], preferred_element_type=f32)
        ).astype(bf16)
        for g in every
    ]
    white = [jnp.dot(err[g], factor[g], preferred_element_type=f32) for g in every]
    live = [(g < count).astype(f32) for g in every]
    weighted = [(live[g] * tau_col * white[g]).astype(bf16) for g in every]
    squares = live[0] * white[0] * white[0]
    for g in range(1, nbd):
        squares = squares + live[g] * white[g] * white[g]
    adj = [lax.dot_general(weighted[g], factor[g], nt, preferred_element_type=f32) for g in every]
    for g in every:
        out_ref[g] = adj[g]
        adjoint[g] = adj[g].astype(bf16)

    live_lane = lax.broadcasted_iota(i32, (1, LANES), 1) == chans
    sums = jnp.sum(
        jnp.where(eye, jnp.sum(squares, axis=1, keepdims=True), 0.0), axis=0, keepdims=True
    )
    sums = sums + jnp.where(live_lane, jnp.minimum(count, nbd).astype(f32), 0.0)
    sq_send[...] = sums

    def share(peer, mine):
        return to_block(sq_send, sq_recv.at[mine], sq_ss.at[peer], sq_rs.at[mine], peer)

    each_peer(lambda peer: share(peer, me).start())
    sq_recv[me] = sums

    for g in every:
        back[g] = lax.dot_general(
            adjoint[g], predict[g, 0], nt, preferred_element_type=f32
        ).astype(bf16)

    def placed(peer):
        got = jnp.dot(place[peer], back[...].reshape(rows, width), preferred_element_type=f32)
        return got.astype(bf16)

    def give(peer, mine):
        return to_block(ret_send.at[peer], ret_recv.at[mine], ret_ss.at[peer], ret_rs.at[mine], peer)

    def give_back(peer):
        ret_send[peer] = placed(peer)
        give(peer, me).start()

    each_peer(give_back)
    ret_recv[me] = placed(me)

    @pl.when(has_prev)
    def _():
        for g in range(nbd):
            seam_ret[g] = lax.dot_general(
                adjoint[g], predict[g, 1], nt, preferred_element_type=f32
            ).astype(bf16)
        seam_bwd.start()

    each_peer(lambda peer: share(me, peer).wait_recv())
    line = sq_recv[0]
    for d in range(1, nblock):
        line = line + sq_recv[d]
    rg_send[...] = line

    def share_region(peer, mine):
        return to_region(rg_send, rg_recv.at[mine], rg_ss.at[peer], rg_rs.at[mine], peer)

    each_region(lambda peer: share_region(peer, region).start())
    rg_recv[region] = line

    @pl.when(has_next)
    def _():
        seam_where_in = to_region(seam_tgt, seam_tgt_in, seam_ss.at[1], seam_rs.at[1], up)
        seam_where_in.wait_recv()
        mask = jnp.where(
            seam_tgt_in[...] == lax.broadcasted_iota(i32, (rows, rows), 0), 1.0, 0.0
        ).astype(bf16)
        seam_bwd.wait_recv()
        got = jnp.dot(mask, seam_ret_in[...].reshape(rows, width), preferred_element_type=f32)
        out_ref[...] = out_ref[...] - got.reshape(nbd, chans, width)

    def add(d):
        got = jnp.dot(spread[d], ret_recv[d], preferred_element_type=f32)
        out_ref[...] = out_ref[...] - got.reshape(nbd, chans, width)

    add(me)

    each_region(lambda peer: share_region(region, peer).wait_recv())
    total = rg_recv[0]
    for r in range(1, nregion):
        total = total + rg_recv[r]
    total_live = jnp.sum(jnp.where(live_lane, total, 0.0), axis=1, keepdims=True)
    blocks = nbd * nblock * nregion
    gtau_ref[...] = (
        0.5 * total[:, :chans] - 0.5 * width * total_live / tau_ref[...]
    ) / (blocks * width)

    def take(peer):
        give(me, peer).wait_recv()
        add(peer)

    each_peer(take)

    def sent(peer):
        request(peer, me).wait_send()
        serve(peer, me).wait_send()
        give(peer, me).wait_send()
        share(peer, me).wait_send()

    each_peer(sent)
    each_region(lambda peer: share_region(peer, region).wait_send())

    @pl.when(has_next)
    def _():
        seam_fwd.wait_send()

    @pl.when(has_prev)
    def _():
        seam_where.wait_send()
        seam_bwd.wait_send()


def shards(obs, predict, factor, tau, nbr_dev, nbr_slot, counts):
    nbd, chans, width = obs.shape
    nblock = lax.axis_size("block")
    nregion = lax.axis_size("region")
    cap = max(2, 2 * nbd // nblock)
    rows = nbd * chans
    part = cap * chans
    lanes = -(-part // LANES) * LANES
    bf16, f32, i32 = jnp.bfloat16, jnp.float32, jnp.int32
    vmem = pl.BlockSpec(memory_space=pltpu.VMEM)
    hbm = pl.BlockSpec(memory_space=pltpu.HBM)
    dma = pltpu.SemaphoreType.DMA
    grad_obs, grad_tau = pl.pallas_call(
        functools.partial(kernel, nblock, nregion, cap),
        out_shape=(
            jax.ShapeDtypeStruct((nbd, chans, width), f32),
            jax.ShapeDtypeStruct((1, chans), f32),
        ),
        in_specs=[hbm] * 7,
        out_specs=(vmem, vmem),
        scratch_shapes=[
            pltpu.SMEM((1, nbd), i32),
            pltpu.SMEM((2, nbd), i32),
            pltpu.SMEM((1,), i32),
            pltpu.VMEM((1, chans), f32),
            pltpu.VMEM((nbd, chans, width), bf16),
            pltpu.VMEM((nbd, 2, width, width), bf16),
            pltpu.VMEM((nbd, width, width), bf16),
            pltpu.VMEM((nblock, 1, lanes), i32),
            pltpu.VMEM((nblock, 1, lanes), i32),
            pltpu.VMEM((nblock * cap, chans, width), bf16),
            pltpu.VMEM((nblock * cap, chans, width), bf16),
            pltpu.VMEM((nblock, part, width), bf16),
            pltpu.VMEM((nblock, part, width), bf16),
            pltpu.VMEM((nbd, chans, width), bf16),
            pltpu.VMEM((1, rows), i32),
            pltpu.VMEM((1, rows), i32),
            pltpu.VMEM((nbd, chans, width), bf16),
            pltpu.VMEM((nbd, chans, width), bf16),
            pltpu.VMEM((nblock, part, rows), bf16),
            pltpu.VMEM((nblock, rows, part), bf16),
            pltpu.VMEM((nbd, chans, width), f32),
            pltpu.VMEM((nbd, chans, width), bf16),
            pltpu.VMEM((nbd, chans, width), bf16),
            pltpu.VMEM((1, LANES), f32),
            pltpu.VMEM((nblock, 1, LANES), f32),
            pltpu.VMEM((1, LANES), f32),
            pltpu.VMEM((nregion, 1, LANES), f32),
            dma((7,)),
            dma((nblock,)),
            dma((nblock,)),
            dma((nblock,)),
            dma((nblock,)),
            dma((nblock,)),
            dma((nblock,)),
            dma((nblock,)),
            dma((nblock,)),
            dma((nregion,)),
            dma((nregion,)),
            dma((3,)),
            dma((3,)),
        ],
        compiler_params=pltpu.CompilerParams(
            collective_id=0, has_side_effects=True
        ),
        name="vecchia",
    )(nbr_dev.T, nbr_slot.T, counts, tau.reshape(1, chans), obs, predict, factor)
    return grad_obs, grad_tau.reshape(chans)


def solution(mesh):
    in_specs = (
        P(("region", "block"), None, None),
        P(("region", "block"), None, None, None),
        P(("region", "block"), None, None),
        P(),
        P(("region", "block"), None),
        P(("region", "block"), None),
        P(("region", "block")),
    )
    out_specs = (P(("region", "block"), None, None), P())
    return jax.shard_map(shards, mesh=mesh, in_specs=in_specs, out_specs=out_specs, check_vma=False)
```

```python
import functools

import jax
import jax.numpy as jnp
from jax import lax
from jax.experimental import pallas as pl
from jax.experimental.pallas import tpu as pltpu
from jax.sharding import PartitionSpec as P

MESH = pl.DeviceIdType.MESH
LANES = 128


def kernel(
    nblock,
    nregion,
    cap,
    dev_hbm,
    slot_hbm,
    counts_hbm,
    tau_hbm,
    obs_hbm,
    predict_hbm,
    factor_hbm,
    out_ref,
    gtau_ref,
    dev_ref,
    slot_ref,
    counts_ref,
    tau_ref,
    obs,
    predict,
    factor,
    req_send,
    req_recv,
    near_send,
    near_recv,
    ret_send,
    ret_recv,
    seam_obs,
    seam_tgt,
    seam_tgt_in,
    seam_ret,
    seam_ret_in,
    held,
    held_ref,
    spread,
    partial,
    back,
    adjoint,
    sq_send,
    sq_recv,
    rg_send,
    rg_recv,
    local_sem,
    req_ss,
    req_rs,
    near_ss,
    near_rs,
    ret_ss,
    ret_rs,
    sq_ss,
    sq_rs,
    rg_ss,
    rg_rs,
    seam_ss,
    seam_rs,
):
    nbd, chans, width = obs.shape
    rows = nbd * chans
    part = cap * chans
    lanes = req_send.shape[2]
    group = 2 if nblock % 2 == 0 and part % LANES == 0 else 1
    me = lax.axis_index("block")
    region = lax.axis_index("region")
    bf16, f32, i32 = jnp.bfloat16, jnp.float32, jnp.int32

    half = me // (nblock // 2)

    def farthest(turn):
        below = nblock - 1 - turn - (me + turn + 1) // nblock
        above = turn + (turn - me + nblock) // nblock
        return below + half * (above - below)

    def each_peer(body, nearest=False):
        def visit(turn):
            body(farthest(nblock - 2 - turn if nearest else turn))

        if nblock <= 8:
            for turn in range(nblock - 1):
                visit(turn)
        else:

            def run(turn, carry):
                visit(turn)
                return carry

            lax.fori_loop(0, nblock - 1, run, 0)

    def each_region(body):
        for step in range(1, nregion):
            body(lax.rem(region + step, nregion))

    def to_block(src, dst, ss, rs, peer):
        return pltpu.make_async_remote_copy(
            src_ref=src,
            dst_ref=dst,
            send_sem=ss,
            recv_sem=rs,
            device_id={"block": peer},
            device_id_type=MESH,
        )

    def to_region(src, dst, ss, rs, peer):
        return pltpu.make_async_remote_copy(
            src_ref=src,
            dst_ref=dst,
            send_sem=ss,
            recv_sem=rs,
            device_id={"region": peer},
            device_id_type=MESH,
        )

    small = [
        pltpu.make_async_copy(src, dst, local_sem.at[3 + i])
        for i, (src, dst) in enumerate(
            [(dev_hbm, dev_ref), (slot_hbm, slot_ref), (counts_hbm, counts_ref), (tau_hbm, tau_ref)]
        )
    ]
    for copy in small:
        copy.start()

    barrier = pltpu.get_barrier_semaphore()
    each_peer(
        lambda peer: pl.semaphore_signal(
            barrier, inc=1, device_id={"block": peer}, device_id_type=MESH
        )
    )
    each_region(
        lambda peer: pl.semaphore_signal(
            barrier, inc=1, device_id={"region": peer}, device_id_type=MESH
        )
    )
    load_obs = pltpu.make_async_copy(obs_hbm, obs, local_sem.at[0])
    load_predict = pltpu.make_async_copy(predict_hbm, predict, local_sem.at[1])
    load_factor = pltpu.make_async_copy(factor_hbm, factor, local_sem.at[2])
    load_obs.start()
    load_predict.start()
    load_factor.start()

    for copy in small:
        copy.wait()

    dest = [dev_ref[0, h] for h in range(nbd)]
    flat = []
    for h in range(nbd):
        rank = jnp.int32(0)
        for g in range(h):
            rank = rank + (dest[g] == dest[h]).astype(i32)
        flat.append(dest[h] * cap + rank)

    lane = lax.broadcasted_iota(i32, (nblock, lanes), 1)
    spot = lax.broadcasted_iota(i32, (nblock, lanes), 0) * cap + lane // chans
    spot = jnp.where(lane < part, spot, -1)
    wanted = jnp.full((nblock, lanes), -1, i32)
    for h in range(nbd):
        wanted = jnp.where(spot == flat[h], slot_ref[0, h] * chans + lane % chans, wanted)
    for d in range(nblock):
        req_send[d] = wanted[d : d + 1]

    block_lane = lax.broadcasted_iota(i32, (1, rows), 1)
    owner_of = block_lane // chans
    seam_row = jnp.zeros((1, rows), i32)
    for h in range(nbd):
        seam_row = jnp.where(owner_of == h, slot_ref[1, h], seam_row)
    seam_tgt[...] = seam_row * chans + block_lane % chans

    place_lane = lax.broadcasted_iota(i32, (1, LANES), 1)
    holder = jnp.full((1, LANES), nbd, i32)
    for h in range(nbd):
        holder = jnp.where(place_lane == flat[h], h, holder)
    held[...] = holder
    load_held = pltpu.make_async_copy(held, held_ref, local_sem.at[7])
    load_held.start()
    back[nbd] = jnp.zeros((chans, width), bf16)

    pl.semaphore_wait(barrier, nblock - 1 + nregion - 1)

    def request(peer, mine):
        return to_block(req_send.at[peer], req_recv.at[mine], req_ss.at[peer], req_rs.at[mine], peer)

    each_peer(lambda peer: request(peer, me).start())
    req_recv[me] = req_send[me]

    down = lax.rem(region + 1, nregion)
    up = lax.rem(region + nregion - 1, nregion)
    seam_fwd = to_region(obs_hbm, seam_obs, seam_ss.at[0], seam_rs.at[0], down)
    seam_where = to_region(seam_tgt, seam_tgt_in, seam_ss.at[1], seam_rs.at[1], up)
    seam_bwd = to_region(seam_ret, seam_ret_in, seam_ss.at[2], seam_rs.at[2], up)
    has_prev = region > 0
    has_next = region < nregion - 1

    @pl.when(has_next)
    def _():
        seam_fwd.start()

    @pl.when(has_prev)
    def _():
        seam_where.start()

    load_obs.wait()
    pick_lane = lax.broadcasted_iota(i32, (part, rows), 1)

    def picked(peer):
        row = jnp.broadcast_to(req_recv[peer], (LANES, lanes))
        column = jnp.transpose(row)[:part]
        column = jnp.concatenate([column] * (rows // LANES), axis=1)
        mask = jnp.where(column == pick_lane, 1.0, 0.0).astype(bf16)
        got = jnp.dot(mask, obs[...].reshape(rows, width), preferred_element_type=f32)
        return got.astype(bf16).reshape(cap, chans, width)

    def span(d):
        return pl.ds(d * cap, cap)

    def serve(peer, mine):
        return to_block(
            near_send.at[span(peer)],
            near_recv.at[span(mine)],
            near_ss.at[peer],
            near_rs.at[mine],
            peer,
        )

    def answer(peer):
        request(me, peer).wait_recv()
        near_send[span(peer)] = picked(peer)
        serve(peer, me).start()

    each_peer(answer, nearest=True)
    near_recv[span(me)] = picked(me)

    def build(chip):
        wanted_row = jnp.concatenate(
            [req_recv[chip * group + i][:, :part] for i in range(group)], axis=1
        )
        spread[chip] = jnp.where(
            wanted_row == lax.broadcasted_iota(i32, (rows, group * part), 0), 1.0, 0.0
        ).astype(bf16)

    for chip in range(nblock // group):
        build(chip)
    load_held.wait()

    @pl.when(has_prev)
    def _():
        seam_fwd.wait_recv()

    @pl.when(jnp.logical_not(has_prev))
    def _():
        seam_obs[...] = jnp.zeros_like(seam_obs)

    load_predict.wait()
    for g in range(nbd):
        partial[g] = obs[g].astype(f32) - jnp.dot(
            seam_obs[slot_ref[1, g]], predict[g, 1], preferred_element_type=f32
        )
    load_factor.wait()

    eye = lax.broadcasted_iota(i32, (chans, LANES), 0) == lax.broadcasted_iota(
        i32, (chans, LANES), 1
    )
    tau_row = jnp.concatenate([tau_ref[...], jnp.zeros((1, LANES - chans), f32)], axis=1)
    tau_col = jnp.sum(jnp.where(eye, tau_row, 0.0), axis=1, keepdims=True)
    count = counts_ref[0]

    each_peer(lambda peer: serve(me, peer).wait_recv())

    nt = (((1,), (1,)), ((), ()))
    every = range(nbd)
    err = [
        (
            partial[g]
            - jnp.dot(near_recv[flat[g]], predict[g, 0], preferred_element_type=f32)
        ).astype(bf16)
        for g in every
    ]
    white = [jnp.dot(err[g], factor[g], preferred_element_type=f32) for g in every]
    live = [(g < count).astype(f32) for g in every]
    weighted = [(live[g] * tau_col * white[g]).astype(bf16) for g in every]
    squares = live[0] * white[0] * white[0]
    for g in range(1, nbd):
        squares = squares + live[g] * white[g] * white[g]
    live_lane = lax.broadcasted_iota(i32, (1, LANES), 1) == chans
    sums = jnp.sum(
        jnp.where(eye, jnp.sum(squares, axis=1, keepdims=True), 0.0), axis=0, keepdims=True
    )
    sums = sums + jnp.where(live_lane, jnp.minimum(count, nbd).astype(f32), 0.0)
    sq_send[...] = sums

    def share(peer, mine):
        return to_block(sq_send, sq_recv.at[mine], sq_ss.at[peer], sq_rs.at[mine], peer)

    each_peer(lambda peer: share(peer, me).start())
    sq_recv[me] = sums

    adj = [lax.dot_general(weighted[g], factor[g], nt, preferred_element_type=f32) for g in every]
    for g in every:
        out_ref[g] = adj[g]
        adjoint[g] = adj[g].astype(bf16)

    for g in every:
        back[g] = lax.dot_general(
            adjoint[g], predict[g, 0], nt, preferred_element_type=f32
        ).astype(bf16)

    def pack(dst, peer):
        for k in range(cap):
            dst[k * chans : (k + 1) * chans] = back[held_ref[0, peer * cap + k]]

    def give(peer, mine):
        return to_block(ret_send.at[peer], ret_recv.at[mine], ret_ss.at[peer], ret_rs.at[mine], peer)

    def give_back(peer):
        pack(ret_send.at[peer], peer)
        give(peer, me).start()

    each_peer(give_back)
    pack(ret_recv.at[me], me)

    @pl.when(has_prev)
    def _():
        for g in range(nbd):
            seam_ret[g] = lax.dot_general(
                adjoint[g], predict[g, 1], nt, preferred_element_type=f32
            ).astype(bf16)
        seam_bwd.start()

    each_peer(lambda peer: share(me, peer).wait_recv(), nearest=True)
    line = sq_recv[0]
    for d in range(1, nblock):
        line = line + sq_recv[d]
    rg_send[...] = line

    def share_region(peer, mine):
        return to_region(rg_send, rg_recv.at[mine], rg_ss.at[peer], rg_rs.at[mine], peer)

    each_region(lambda peer: share_region(peer, region).start())
    rg_recv[region] = line

    @pl.when(has_next)
    def _():
        seam_where_in = to_region(seam_tgt, seam_tgt_in, seam_ss.at[1], seam_rs.at[1], up)
        seam_where_in.wait_recv()
        mask = jnp.where(
            seam_tgt_in[...] == lax.broadcasted_iota(i32, (rows, rows), 0), 1.0, 0.0
        ).astype(bf16)
        seam_bwd.wait_recv()
        got = jnp.dot(mask, seam_ret_in[...].reshape(rows, width), preferred_element_type=f32)
        out_ref[...] = out_ref[...] - got.reshape(nbd, chans, width)

    def add(chip):
        blocks_back = ret_recv[pl.ds(chip * group, group)].reshape(group * part, width)
        got = jnp.dot(spread[chip], blocks_back, preferred_element_type=f32)
        out_ref[...] = out_ref[...] - got.reshape(nbd, chans, width)

    each_peer(lambda peer: give(me, peer).wait_recv(), nearest=True)
    for chip in range(nblock // group):
        add(chip)

    each_region(lambda peer: share_region(region, peer).wait_recv())
    total = rg_recv[0]
    for r in range(1, nregion):
        total = total + rg_recv[r]
    total_live = jnp.sum(jnp.where(live_lane, total, 0.0), axis=1, keepdims=True)
    blocks = nbd * nblock * nregion
    gtau_ref[...] = (
        0.5 * total[:, :chans] - 0.5 * width * total_live / tau_ref[...]
    ) / (blocks * width)

    def sent(peer):
        request(peer, me).wait_send()
        serve(peer, me).wait_send()
        give(peer, me).wait_send()
        share(peer, me).wait_send()

    each_peer(sent)
    each_region(lambda peer: share_region(peer, region).wait_send())

    @pl.when(has_next)
    def _():
        seam_fwd.wait_send()

    @pl.when(has_prev)
    def _():
        seam_where.wait_send()
        seam_bwd.wait_send()


def shards(obs, predict, factor, tau, nbr_dev, nbr_slot, counts):
    nbd, chans, width = obs.shape
    nblock = lax.axis_size("block")
    nregion = lax.axis_size("region")
    cap = max(2, 2 * nbd // nblock)
    rows = nbd * chans
    part = cap * chans
    lanes = -(-part // LANES) * LANES
    group = 2 if nblock % 2 == 0 and part % LANES == 0 else 1
    bf16, f32, i32 = jnp.bfloat16, jnp.float32, jnp.int32
    vmem = pl.BlockSpec(memory_space=pltpu.VMEM)
    hbm = pl.BlockSpec(memory_space=pltpu.HBM)
    dma = pltpu.SemaphoreType.DMA
    grad_obs, grad_tau = pl.pallas_call(
        functools.partial(kernel, nblock, nregion, cap),
        out_shape=(
            jax.ShapeDtypeStruct((nbd, chans, width), f32),
            jax.ShapeDtypeStruct((1, chans), f32),
        ),
        in_specs=[hbm] * 7,
        out_specs=(vmem, vmem),
        scratch_shapes=[
            pltpu.SMEM((1, nbd), i32),
            pltpu.SMEM((2, nbd), i32),
            pltpu.SMEM((1,), i32),
            pltpu.VMEM((1, chans), f32),
            pltpu.VMEM((nbd, chans, width), bf16),
            pltpu.VMEM((nbd, 2, width, width), bf16),
            pltpu.VMEM((nbd, width, width), bf16),
            pltpu.VMEM((nblock, 1, lanes), i32),
            pltpu.VMEM((nblock, 1, lanes), i32),
            pltpu.VMEM((nblock * cap, chans, width), bf16),
            pltpu.VMEM((nblock * cap, chans, width), bf16),
            pltpu.VMEM((nblock, part, width), bf16),
            pltpu.VMEM((nblock, part, width), bf16),
            pltpu.VMEM((nbd, chans, width), bf16),
            pltpu.VMEM((1, rows), i32),
            pltpu.VMEM((1, rows), i32),
            pltpu.VMEM((nbd, chans, width), bf16),
            pltpu.VMEM((nbd, chans, width), bf16),
            pltpu.VMEM((1, LANES), i32),
            pltpu.SMEM((1, LANES), i32),
            pltpu.VMEM((nblock // group, rows, group * part), bf16),
            pltpu.VMEM((nbd, chans, width), f32),
            pltpu.VMEM((nbd + 1, chans, width), bf16),
            pltpu.VMEM((nbd, chans, width), bf16),
            pltpu.VMEM((1, LANES), f32),
            pltpu.VMEM((nblock, 1, LANES), f32),
            pltpu.VMEM((1, LANES), f32),
            pltpu.VMEM((nregion, 1, LANES), f32),
            dma((8,)),
            dma((nblock,)),
            dma((nblock,)),
            dma((nblock,)),
            dma((nblock,)),
            dma((nblock,)),
            dma((nblock,)),
            dma((nblock,)),
            dma((nblock,)),
            dma((nregion,)),
            dma((nregion,)),
            dma((3,)),
            dma((3,)),
        ],
        compiler_params=pltpu.CompilerParams(
            collective_id=0, has_side_effects=True
        ),
        name="vecchia",
    )(nbr_dev.T, nbr_slot.T, counts, tau.reshape(1, chans), obs, predict, factor)
    return grad_obs, grad_tau.reshape(chans)


def solution(mesh):
    in_specs = (
        P(("region", "block"), None, None),
        P(("region", "block"), None, None, None),
        P(("region", "block"), None, None),
        P(),
        P(("region", "block"), None),
        P(("region", "block"), None),
        P(("region", "block")),
    )
    out_specs = (P(("region", "block"), None, None), P())
    return jax.shard_map(shards, mesh=mesh, in_specs=in_specs, out_specs=out_specs, check_vma=False)
```

```python
import functools

import jax
import jax.numpy as jnp
from jax import lax
from jax.experimental import pallas as pl
from jax.experimental.pallas import tpu as pltpu
from jax.sharding import PartitionSpec as P

MESH = pl.DeviceIdType.MESH
LANES = 128


def kernel(
    nblock,
    nregion,
    cap,
    dev_hbm,
    slot_hbm,
    counts_hbm,
    tau_hbm,
    obs_hbm,
    predict_hbm,
    factor_hbm,
    out_ref,
    gtau_ref,
    dev_ref,
    slot_ref,
    counts_ref,
    tau_ref,
    obs,
    predict,
    factor,
    req_send,
    req_recv,
    near_send,
    near_recv,
    ret_send,
    ret_recv,
    seam_obs,
    seam_tgt,
    seam_tgt_in,
    seam_ret,
    seam_ret_in,
    held,
    held_ref,
    spread,
    partial,
    back,
    adjoint,
    sq_send,
    sq_recv,
    rg_send,
    rg_recv,
    local_sem,
    req_ss,
    req_rs,
    near_ss,
    near_rs,
    ret_ss,
    ret_rs,
    sq_ss,
    sq_rs,
    rg_ss,
    rg_rs,
    seam_ss,
    seam_rs,
    far_ss,
    far_rs,
):
    nbd, chans, width = obs.shape
    rows = nbd * chans
    part = cap * chans
    lanes = req_send.shape[2]
    group = 2 if nblock % 2 == 0 and part % LANES == 0 else 1
    me = lax.axis_index("block")
    region = lax.axis_index("region")
    bf16, f32, i32 = jnp.bfloat16, jnp.float32, jnp.int32

    half = me // (nblock // 2)

    def farthest(turn):
        below = nblock - 1 - turn - (me + turn + 1) // nblock
        above = turn + (turn - me + nblock) // nblock
        return below + half * (above - below)

    def each_peer(body, nearest=False):
        def visit(turn):
            body(farthest(nblock - 2 - turn if nearest else turn))

        if nblock <= 8:
            for turn in range(nblock - 1):
                visit(turn)
        else:

            def run(turn, carry):
                visit(turn)
                return carry

            lax.fori_loop(0, nblock - 1, run, 0)

    chip, core = me // 2, lax.rem(me, 2)
    across = nblock // 2 - 1 - chip
    whole = nblock * cap
    ends = nblock == 8
    at_end = chip * across == 0

    def far(peer):
        return jnp.logical_and(at_end, peer // 2 == across)

    def each_region(body):
        for step in range(1, nregion):
            body(lax.rem(region + step, nregion))

    def to_block(src, dst, ss, rs, peer):
        return pltpu.make_async_remote_copy(
            src_ref=src,
            dst_ref=dst,
            send_sem=ss,
            recv_sem=rs,
            device_id={"block": peer},
            device_id_type=MESH,
        )

    def to_region(src, dst, ss, rs, peer):
        return pltpu.make_async_remote_copy(
            src_ref=src,
            dst_ref=dst,
            send_sem=ss,
            recv_sem=rs,
            device_id={"region": peer},
            device_id_type=MESH,
        )

    if ends:

        @pl.when(jnp.logical_not(at_end))
        def _():
            near_recv[whole:] = jnp.zeros((2 * nbd, chans, width), bf16)

        @pl.when(at_end)
        def _():
            near_recv[pl.ds(across * 2 * cap, 2 * cap)] = jnp.zeros((2 * cap, chans, width), bf16)

    small = [
        pltpu.make_async_copy(src, dst, local_sem.at[3 + i])
        for i, (src, dst) in enumerate(
            [(dev_hbm, dev_ref), (slot_hbm, slot_ref), (counts_hbm, counts_ref), (tau_hbm, tau_ref)]
        )
    ]
    for copy in small:
        copy.start()

    barrier = pltpu.get_barrier_semaphore()
    each_peer(
        lambda peer: pl.semaphore_signal(
            barrier, inc=1, device_id={"block": peer}, device_id_type=MESH
        )
    )
    each_region(
        lambda peer: pl.semaphore_signal(
            barrier, inc=1, device_id={"region": peer}, device_id_type=MESH
        )
    )
    load_obs = pltpu.make_async_copy(obs_hbm, obs, local_sem.at[0])
    load_predict = pltpu.make_async_copy(predict_hbm, predict, local_sem.at[1])
    load_factor = pltpu.make_async_copy(factor_hbm, factor, local_sem.at[2])
    load_obs.start()
    load_predict.start()
    load_factor.start()

    for copy in small:
        copy.wait()

    dest = [dev_ref[0, h] for h in range(nbd)]
    flat = []
    for h in range(nbd):
        rank = jnp.int32(0)
        for g in range(h):
            rank = rank + (dest[g] == dest[h]).astype(i32)
        flat.append(dest[h] * cap + rank)

    lane = lax.broadcasted_iota(i32, (nblock, lanes), 1)
    spot = lax.broadcasted_iota(i32, (nblock, lanes), 0) * cap + lane // chans
    spot = jnp.where(lane < part, spot, -1)
    wanted = jnp.full((nblock, lanes), -1, i32)
    for h in range(nbd):
        wanted = jnp.where(spot == flat[h], slot_ref[0, h] * chans + lane % chans, wanted)
    for d in range(nblock):
        req_send[d] = wanted[d : d + 1]

    block_lane = lax.broadcasted_iota(i32, (1, rows), 1)
    owner_of = block_lane // chans
    seam_row = jnp.zeros((1, rows), i32)
    for h in range(nbd):
        seam_row = jnp.where(owner_of == h, slot_ref[1, h], seam_row)
    seam_tgt[...] = seam_row * chans + block_lane % chans

    place_lane = lax.broadcasted_iota(i32, (1, LANES), 1)
    holder = jnp.full((1, LANES), nbd, i32)
    for h in range(nbd):
        holder = jnp.where(place_lane == flat[h], h, holder)
    held[...] = holder
    load_held = pltpu.make_async_copy(held, held_ref, local_sem.at[7])
    load_held.start()
    back[nbd] = jnp.zeros((chans, width), bf16)

    pl.semaphore_wait(barrier, nblock - 1 + nregion - 1)

    def request(peer, mine):
        return to_block(req_send.at[peer], req_recv.at[mine], req_ss.at[peer], req_rs.at[mine], peer)

    each_peer(lambda peer: request(peer, me).start())
    req_recv[me] = req_send[me]

    def far_slot(i):
        return near_recv.at[pl.ds(whole + i * nbd, nbd)]

    far_copy = to_block(obs_hbm, far_slot(core), far_ss.at[0], far_rs.at[0], across * 2 + core)
    relay = to_block(
        far_slot(core), far_slot(core), far_ss.at[1], far_rs.at[1], chip * 2 + 1 - core
    )
    if ends:

        @pl.when(at_end)
        def _():
            far_copy.start()

    down = lax.rem(region + 1, nregion)
    up = lax.rem(region + nregion - 1, nregion)
    seam_fwd = to_region(obs_hbm, seam_obs, seam_ss.at[0], seam_rs.at[0], down)
    seam_where = to_region(seam_tgt, seam_tgt_in, seam_ss.at[1], seam_rs.at[1], up)
    seam_bwd = to_region(seam_ret, seam_ret_in, seam_ss.at[2], seam_rs.at[2], up)
    has_prev = region > 0
    has_next = region < nregion - 1

    @pl.when(has_next)
    def _():
        seam_fwd.start()

    @pl.when(has_prev)
    def _():
        seam_where.start()

    load_obs.wait()
    pick_lane = lax.broadcasted_iota(i32, (part, rows), 1)

    def picked(peer):
        row = jnp.broadcast_to(req_recv[peer], (LANES, lanes))
        column = jnp.transpose(row)[:part]
        column = jnp.concatenate([column] * (rows // LANES), axis=1)
        mask = jnp.where(column == pick_lane, 1.0, 0.0).astype(bf16)
        got = jnp.dot(mask, obs[...].reshape(rows, width), preferred_element_type=f32)
        return got.astype(bf16).reshape(cap, chans, width)

    def span(d):
        return pl.ds(d * cap, cap)

    def serve(peer, mine):
        return to_block(
            near_send.at[span(peer)],
            near_recv.at[span(mine)],
            near_ss.at[peer],
            near_rs.at[mine],
            peer,
        )

    def put(peer):
        near_send[span(peer)] = picked(peer)
        serve(peer, me).start()

    def unless_far(peer, act):
        if ends:
            pl.when(jnp.logical_not(far(peer)))(act)
        else:
            act()

    def answer(peer):
        request(me, peer).wait_recv()
        unless_far(peer, lambda: put(peer))

    each_peer(answer, nearest=True)
    near_recv[span(me)] = picked(me)
    if ends:

        @pl.when(at_end)
        def _():
            far_copy.wait_recv()
            relay.start()


    def build(pair):
        wanted_row = jnp.concatenate(
            [req_recv[pair * group + i][:, :part] for i in range(group)], axis=1
        )
        spread[pair] = jnp.where(
            wanted_row == lax.broadcasted_iota(i32, (rows, group * part), 0), 1.0, 0.0
        ).astype(bf16)

    for pair in range(nblock // group):
        build(pair)
    load_held.wait()

    @pl.when(has_prev)
    def _():
        seam_fwd.wait_recv()

    @pl.when(jnp.logical_not(has_prev))
    def _():
        seam_obs[...] = jnp.zeros_like(seam_obs)

    load_predict.wait()
    for g in range(nbd):
        partial[g] = obs[g].astype(f32) - jnp.dot(
            seam_obs[slot_ref[1, g]], predict[g, 1], preferred_element_type=f32
        )
    load_factor.wait()

    eye = lax.broadcasted_iota(i32, (chans, LANES), 0) == lax.broadcasted_iota(
        i32, (chans, LANES), 1
    )
    tau_row = jnp.concatenate([tau_ref[...], jnp.zeros((1, LANES - chans), f32)], axis=1)
    tau_col = jnp.sum(jnp.where(eye, tau_row, 0.0), axis=1, keepdims=True)
    count = counts_ref[0]

    source = flat
    if ends:
        at_far = [jnp.logical_and(at_end, dest[h] // 2 == across) for h in range(nbd)]
        source = [
            jnp.where(at_far[h], whole + lax.rem(dest[h], 2) * nbd + slot_ref[0, h], flat[h])
            for h in range(nbd)
        ]

        @pl.when(at_end)
        def _():
            relay.wait_recv()

    each_peer(lambda peer: unless_far(peer, lambda: serve(me, peer).wait_recv()), nearest=True)

    nt = (((1,), (1,)), ((), ()))
    every = range(nbd)
    err = [
        (
            partial[g]
            - jnp.dot(near_recv[source[g]], predict[g, 0], preferred_element_type=f32)
        ).astype(bf16)
        for g in every
    ]
    white = [jnp.dot(err[g], factor[g], preferred_element_type=f32) for g in every]
    live = [(g < count).astype(f32) for g in every]
    weighted = [(live[g] * tau_col * white[g]).astype(bf16) for g in every]
    squares = live[0] * white[0] * white[0]
    for g in range(1, nbd):
        squares = squares + live[g] * white[g] * white[g]
    live_lane = lax.broadcasted_iota(i32, (1, LANES), 1) == chans
    sums = jnp.sum(
        jnp.where(eye, jnp.sum(squares, axis=1, keepdims=True), 0.0), axis=0, keepdims=True
    )
    sums = sums + jnp.where(live_lane, jnp.minimum(count, nbd).astype(f32), 0.0)
    sq_send[...] = sums

    def share(peer, mine):
        return to_block(sq_send, sq_recv.at[mine], sq_ss.at[peer], sq_rs.at[mine], peer)

    each_peer(lambda peer: share(peer, me).start())
    sq_recv[me] = sums

    adj = [lax.dot_general(weighted[g], factor[g], nt, preferred_element_type=f32) for g in every]
    for g in every:
        out_ref[g] = adj[g]
        adjoint[g] = adj[g].astype(bf16)

    for g in every:
        back[g] = lax.dot_general(
            adjoint[g], predict[g, 0], nt, preferred_element_type=f32
        ).astype(bf16)

    def pack(dst, peer):
        for k in range(cap):
            dst[k * chans : (k + 1) * chans] = back[held_ref[0, peer * cap + k]]

    def give(peer, mine):
        return to_block(ret_send.at[peer], ret_recv.at[mine], ret_ss.at[peer], ret_rs.at[mine], peer)

    def give_back(peer):
        pack(ret_send.at[peer], peer)
        give(peer, me).start()

    each_peer(give_back)
    pack(ret_recv.at[me], me)

    @pl.when(has_prev)
    def _():
        for g in range(nbd):
            seam_ret[g] = lax.dot_general(
                adjoint[g], predict[g, 1], nt, preferred_element_type=f32
            ).astype(bf16)
        seam_bwd.start()

    each_peer(lambda peer: share(me, peer).wait_recv(), nearest=True)
    line = sq_recv[0]
    for d in range(1, nblock):
        line = line + sq_recv[d]
    rg_send[...] = line

    def share_region(peer, mine):
        return to_region(rg_send, rg_recv.at[mine], rg_ss.at[peer], rg_rs.at[mine], peer)

    each_region(lambda peer: share_region(peer, region).start())
    rg_recv[region] = line

    @pl.when(has_next)
    def _():
        seam_where_in = to_region(seam_tgt, seam_tgt_in, seam_ss.at[1], seam_rs.at[1], up)
        seam_where_in.wait_recv()
        mask = jnp.where(
            seam_tgt_in[...] == lax.broadcasted_iota(i32, (rows, rows), 0), 1.0, 0.0
        ).astype(bf16)
        seam_bwd.wait_recv()
        got = jnp.dot(mask, seam_ret_in[...].reshape(rows, width), preferred_element_type=f32)
        out_ref[...] = out_ref[...] - got.reshape(nbd, chans, width)

    def add(pair):
        blocks_back = ret_recv[pl.ds(pair * group, group)].reshape(group * part, width)
        got = jnp.dot(spread[pair], blocks_back, preferred_element_type=f32)
        out_ref[...] = out_ref[...] - got.reshape(nbd, chans, width)

    each_peer(lambda peer: give(me, peer).wait_recv(), nearest=True)
    for pair in range(nblock // group):
        add(pair)

    each_region(lambda peer: share_region(region, peer).wait_recv())
    total = rg_recv[0]
    for r in range(1, nregion):
        total = total + rg_recv[r]
    total_live = jnp.sum(jnp.where(live_lane, total, 0.0), axis=1, keepdims=True)
    blocks = nbd * nblock * nregion
    gtau_ref[...] = (
        0.5 * total[:, :chans] - 0.5 * width * total_live / tau_ref[...]
    ) / (blocks * width)

    def sent(peer):
        request(peer, me).wait_send()
        unless_far(peer, lambda: serve(peer, me).wait_send())
        give(peer, me).wait_send()
        share(peer, me).wait_send()

    each_peer(sent)
    if ends:

        @pl.when(at_end)
        def _():
            far_copy.wait_send()
            relay.wait_send()

    each_region(lambda peer: share_region(peer, region).wait_send())

    @pl.when(has_next)
    def _():
        seam_fwd.wait_send()

    @pl.when(has_prev)
    def _():
        seam_where.wait_send()
        seam_bwd.wait_send()


def shards(obs, predict, factor, tau, nbr_dev, nbr_slot, counts):
    nbd, chans, width = obs.shape
    nblock = lax.axis_size("block")
    nregion = lax.axis_size("region")
    cap = max(2, 2 * nbd // nblock)
    rows = nbd * chans
    part = cap * chans
    lanes = -(-part // LANES) * LANES
    group = 2 if nblock % 2 == 0 and part % LANES == 0 else 1
    bf16, f32, i32 = jnp.bfloat16, jnp.float32, jnp.int32
    vmem = pl.BlockSpec(memory_space=pltpu.VMEM)
    hbm = pl.BlockSpec(memory_space=pltpu.HBM)
    dma = pltpu.SemaphoreType.DMA
    grad_obs, grad_tau = pl.pallas_call(
        functools.partial(kernel, nblock, nregion, cap),
        out_shape=(
            jax.ShapeDtypeStruct((nbd, chans, width), f32),
            jax.ShapeDtypeStruct((1, chans), f32),
        ),
        in_specs=[hbm] * 7,
        out_specs=(vmem, vmem),
        scratch_shapes=[
            pltpu.SMEM((1, nbd), i32),
            pltpu.SMEM((2, nbd), i32),
            pltpu.SMEM((1,), i32),
            pltpu.VMEM((1, chans), f32),
            pltpu.VMEM((nbd, chans, width), bf16),
            pltpu.VMEM((nbd, 2, width, width), bf16),
            pltpu.VMEM((nbd, width, width), bf16),
            pltpu.VMEM((nblock, 1, lanes), i32),
            pltpu.VMEM((nblock, 1, lanes), i32),
            pltpu.VMEM((nblock * cap, chans, width), bf16),
            pltpu.VMEM((nblock * cap + 2 * nbd, chans, width), bf16),
            pltpu.VMEM((nblock, part, width), bf16),
            pltpu.VMEM((nblock, part, width), bf16),
            pltpu.VMEM((nbd, chans, width), bf16),
            pltpu.VMEM((1, rows), i32),
            pltpu.VMEM((1, rows), i32),
            pltpu.VMEM((nbd, chans, width), bf16),
            pltpu.VMEM((nbd, chans, width), bf16),
            pltpu.VMEM((1, LANES), i32),
            pltpu.SMEM((1, LANES), i32),
            pltpu.VMEM((nblock // group, rows, group * part), bf16),
            pltpu.VMEM((nbd, chans, width), f32),
            pltpu.VMEM((nbd + 1, chans, width), bf16),
            pltpu.VMEM((nbd, chans, width), bf16),
            pltpu.VMEM((1, LANES), f32),
            pltpu.VMEM((nblock, 1, LANES), f32),
            pltpu.VMEM((1, LANES), f32),
            pltpu.VMEM((nregion, 1, LANES), f32),
            dma((8,)),
            dma((nblock,)),
            dma((nblock,)),
            dma((nblock,)),
            dma((nblock,)),
            dma((nblock,)),
            dma((nblock,)),
            dma((nblock,)),
            dma((nblock,)),
            dma((nregion,)),
            dma((nregion,)),
            dma((3,)),
            dma((3,)),
            dma((2,)),
            dma((2,)),
        ],
        compiler_params=pltpu.CompilerParams(
            collective_id=0, has_side_effects=True
        ),
        name="vecchia",
    )(nbr_dev.T, nbr_slot.T, counts, tau.reshape(1, chans), obs, predict, factor)
    return grad_obs, grad_tau.reshape(chans)


def solution(mesh):
    in_specs = (
        P(("region", "block"), None, None),
        P(("region", "block"), None, None, None),
        P(("region", "block"), None, None),
        P(),
        P(("region", "block"), None),
        P(("region", "block"), None),
        P(("region", "block")),
    )
    out_specs = (P(("region", "block"), None, None), P())
    return jax.shard_map(shards, mesh=mesh, in_specs=in_specs, out_specs=out_specs, check_vma=False)
```

```python
import functools

import jax
import jax.numpy as jnp
from jax import lax
from jax.experimental import pallas as pl
from jax.experimental.pallas import tpu as pltpu
from jax.sharding import PartitionSpec as P

MESH = pl.DeviceIdType.MESH
LANES = 128


def kernel(
    nblock,
    nregion,
    cap,
    dev_hbm,
    slot_hbm,
    counts_hbm,
    tau_hbm,
    obs_hbm,
    predict_hbm,
    factor_hbm,
    out_ref,
    gtau_ref,
    dev_ref,
    slot_ref,
    counts_ref,
    tau_ref,
    obs,
    predict,
    factor,
    req_send,
    req_recv,
    near_send,
    near_recv,
    ret_send,
    ret_recv,
    seam_obs,
    seam_tgt,
    seam_tgt_in,
    seam_ret,
    seam_ret_in,
    held,
    held_ref,
    spread,
    partial,
    back,
    adjoint,
    sq_send,
    sq_recv,
    rg_send,
    rg_recv,
    local_sem,
    req_ss,
    req_rs,
    near_ss,
    near_rs,
    ret_ss,
    ret_rs,
    sq_ss,
    sq_rs,
    rg_ss,
    rg_rs,
    seam_ss,
    seam_rs,
    far_ss,
    far_rs,
):
    nbd, chans, width = obs.shape
    rows = nbd * chans
    part = cap * chans
    lanes = req_send.shape[2]
    group = 2 if nblock % 2 == 0 and part % LANES == 0 else 1
    me = lax.axis_index("block")
    region = lax.axis_index("region")
    bf16, f32, i32 = jnp.bfloat16, jnp.float32, jnp.int32

    half = me // (nblock // 2)

    def farthest(turn):
        below = nblock - 1 - turn - (me + turn + 1) // nblock
        above = turn + (turn - me + nblock) // nblock
        return below + half * (above - below)

    def each_peer(body, nearest=False):
        def visit(turn):
            body(farthest(nblock - 2 - turn if nearest else turn))

        if nblock <= 8:
            for turn in range(nblock - 1):
                visit(turn)
        else:

            def run(turn, carry):
                visit(turn)
                return carry

            lax.fori_loop(0, nblock - 1, run, 0)

    chip, core = me // 2, lax.rem(me, 2)
    across = nblock // 2 - 1 - chip
    whole = nblock * cap
    ends = nblock == 8
    at_end = chip * across == 0

    def far(peer):
        return jnp.logical_and(at_end, peer // 2 == across)

    def each_region(body):
        for step in range(1, nregion):
            body(lax.rem(region + step, nregion))

    def to_block(src, dst, ss, rs, peer):
        return pltpu.make_async_remote_copy(
            src_ref=src,
            dst_ref=dst,
            send_sem=ss,
            recv_sem=rs,
            device_id={"block": peer},
            device_id_type=MESH,
        )

    def to_region(src, dst, ss, rs, peer):
        return pltpu.make_async_remote_copy(
            src_ref=src,
            dst_ref=dst,
            send_sem=ss,
            recv_sem=rs,
            device_id={"region": peer},
            device_id_type=MESH,
        )

    if ends:

        @pl.when(jnp.logical_not(at_end))
        def _():
            near_recv[whole:] = jnp.zeros((2 * nbd, chans, width), bf16)

        @pl.when(at_end)
        def _():
            near_recv[pl.ds(across * 2 * cap, 2 * cap)] = jnp.zeros((2 * cap, chans, width), bf16)

    small = [
        pltpu.make_async_copy(src, dst, local_sem.at[3 + i])
        for i, (src, dst) in enumerate(
            [(dev_hbm, dev_ref), (slot_hbm, slot_ref), (counts_hbm, counts_ref), (tau_hbm, tau_ref)]
        )
    ]
    for copy in small:
        copy.start()

    barrier = pltpu.get_barrier_semaphore()
    each_peer(
        lambda peer: pl.semaphore_signal(
            barrier, inc=1, device_id={"block": peer}, device_id_type=MESH
        )
    )
    each_region(
        lambda peer: pl.semaphore_signal(
            barrier, inc=1, device_id={"region": peer}, device_id_type=MESH
        )
    )
    load_obs = pltpu.make_async_copy(obs_hbm, obs, local_sem.at[0])
    load_predict = pltpu.make_async_copy(predict_hbm, predict, local_sem.at[1])
    load_factor = pltpu.make_async_copy(factor_hbm, factor, local_sem.at[2])
    load_obs.start()
    load_predict.start()
    load_factor.start()

    for copy in small:
        copy.wait()

    dest = [dev_ref[0, h] for h in range(nbd)]
    flat = []
    for h in range(nbd):
        rank = jnp.int32(0)
        for g in range(h):
            rank = rank + (dest[g] == dest[h]).astype(i32)
        flat.append(dest[h] * cap + rank)

    lane = lax.broadcasted_iota(i32, (nblock, lanes), 1)
    spot = lax.broadcasted_iota(i32, (nblock, lanes), 0) * cap + lane // chans
    spot = jnp.where(lane < part, spot, -1)
    wanted = jnp.full((nblock, lanes), -1, i32)
    for h in range(nbd):
        wanted = jnp.where(spot == flat[h], slot_ref[0, h] * chans + lane % chans, wanted)
    for d in range(nblock):
        req_send[d] = wanted[d : d + 1]

    block_lane = lax.broadcasted_iota(i32, (1, rows), 1)
    owner_of = block_lane // chans
    seam_row = jnp.zeros((1, rows), i32)
    for h in range(nbd):
        seam_row = jnp.where(owner_of == h, slot_ref[1, h], seam_row)
    seam_tgt[...] = seam_row * chans + block_lane % chans

    place_lane = lax.broadcasted_iota(i32, (1, LANES), 1)
    holder = jnp.full((1, LANES), nbd, i32)
    for h in range(nbd):
        holder = jnp.where(place_lane == flat[h], h, holder)
    held[...] = holder
    load_held = pltpu.make_async_copy(held, held_ref, local_sem.at[7])
    load_held.start()
    back[nbd] = jnp.zeros((chans, width), bf16)

    pl.semaphore_wait(barrier, nblock - 1 + nregion - 1)

    def request(peer, mine):
        return to_block(req_send.at[peer], req_recv.at[mine], req_ss.at[peer], req_rs.at[mine], peer)

    each_peer(lambda peer: request(peer, me).start())
    req_recv[me] = req_send[me]

    def far_slot(i):
        return near_recv.at[pl.ds(whole + i * nbd, nbd)]

    far_copy = to_block(obs_hbm, far_slot(core), far_ss.at[0], far_rs.at[0], across * 2 + core)
    relay = to_block(
        far_slot(core), far_slot(core), far_ss.at[1], far_rs.at[1], chip * 2 + 1 - core
    )
    if ends:

        @pl.when(at_end)
        def _():
            far_copy.start()

    down = lax.rem(region + 1, nregion)
    up = lax.rem(region + nregion - 1, nregion)
    seam_fwd = to_region(obs_hbm, seam_obs, seam_ss.at[0], seam_rs.at[0], down)
    seam_where = to_region(seam_tgt, seam_tgt_in, seam_ss.at[1], seam_rs.at[1], up)
    seam_bwd = to_region(seam_ret, seam_ret_in, seam_ss.at[2], seam_rs.at[2], up)
    has_prev = region > 0
    has_next = region < nregion - 1

    @pl.when(has_next)
    def _():
        seam_fwd.start()

    @pl.when(has_prev)
    def _():
        seam_where.start()

    load_obs.wait()
    pick_lane = lax.broadcasted_iota(i32, (part, rows), 1)

    def picked(peer):
        row = jnp.broadcast_to(req_recv[peer], (LANES, lanes))
        column = jnp.transpose(row)[:part]
        column = jnp.concatenate([column] * (rows // LANES), axis=1)
        mask = jnp.where(column == pick_lane, 1.0, 0.0).astype(bf16)
        got = jnp.dot(mask, obs[...].reshape(rows, width), preferred_element_type=f32)
        return got.astype(bf16).reshape(cap, chans, width)

    def span(d):
        return pl.ds(d * cap, cap)

    def serve(peer, mine):
        return to_block(
            near_send.at[span(peer)],
            near_recv.at[span(mine)],
            near_ss.at[peer],
            near_rs.at[mine],
            peer,
        )

    def put(peer):
        near_send[span(peer)] = picked(peer)
        serve(peer, me).start()

    def unless_far(peer, act):
        if ends:
            pl.when(jnp.logical_not(far(peer)))(act)
        else:
            act()

    def answer(peer):
        request(me, peer).wait_recv()
        unless_far(peer, lambda: put(peer))

    each_peer(answer, nearest=True)
    near_recv[span(me)] = picked(me)
    if ends:

        @pl.when(at_end)
        def _():
            far_copy.wait_recv()
            relay.start()


    def build(pair):
        wanted_row = jnp.concatenate(
            [req_recv[pair * group + i][:, :part] for i in range(group)], axis=1
        )
        spread[pair] = jnp.where(
            wanted_row == lax.broadcasted_iota(i32, (rows, group * part), 0), 1.0, 0.0
        ).astype(bf16)

    for pair in range(nblock // group):
        build(pair)
    load_held.wait()

    @pl.when(has_prev)
    def _():
        seam_fwd.wait_recv()

    @pl.when(jnp.logical_not(has_prev))
    def _():
        seam_obs[...] = jnp.zeros_like(seam_obs)

    load_predict.wait()
    for g in range(nbd):
        partial[g] = obs[g].astype(f32) - jnp.dot(
            seam_obs[slot_ref[1, g]], predict[g, 1], preferred_element_type=f32
        )
    load_factor.wait()

    eye = lax.broadcasted_iota(i32, (chans, LANES), 0) == lax.broadcasted_iota(
        i32, (chans, LANES), 1
    )
    tau_row = jnp.concatenate([tau_ref[...], jnp.zeros((1, LANES - chans), f32)], axis=1)
    tau_col = jnp.sum(jnp.where(eye, tau_row, 0.0), axis=1, keepdims=True)
    count = counts_ref[0]

    source = flat
    if ends:
        at_far = [jnp.logical_and(at_end, dest[h] // 2 == across) for h in range(nbd)]
        source = [
            jnp.where(at_far[h], whole + lax.rem(dest[h], 2) * nbd + slot_ref[0, h], flat[h])
            for h in range(nbd)
        ]

        @pl.when(at_end)
        def _():
            relay.wait_recv()

    each_peer(lambda peer: unless_far(peer, lambda: serve(me, peer).wait_recv()), nearest=True)

    nt = (((1,), (1,)), ((), ()))
    every = range(nbd)
    err = [
        (
            partial[g]
            - jnp.dot(near_recv[source[g]], predict[g, 0], preferred_element_type=f32)
        ).astype(bf16)
        for g in every
    ]
    white = [jnp.dot(err[g], factor[g], preferred_element_type=f32) for g in every]
    live = [(g < count).astype(f32) for g in every]
    weighted = [(live[g] * tau_col * white[g]).astype(bf16) for g in every]
    squares = live[0] * white[0] * white[0]
    for g in range(1, nbd):
        squares = squares + live[g] * white[g] * white[g]
    live_lane = lax.broadcasted_iota(i32, (1, LANES), 1) == chans
    sums = jnp.sum(
        jnp.where(eye, jnp.sum(squares, axis=1, keepdims=True), 0.0), axis=0, keepdims=True
    )
    sums = sums + jnp.where(live_lane, jnp.minimum(count, nbd).astype(f32), 0.0)
    sq_send[...] = sums

    def share(peer, mine):
        return to_block(sq_send, sq_recv.at[mine], sq_ss.at[peer], sq_rs.at[mine], peer)

    each_peer(lambda peer: share(peer, me).start())
    sq_recv[me] = sums

    adj = [lax.dot_general(weighted[g], factor[g], nt, preferred_element_type=f32) for g in every]
    for g in every:
        out_ref[g] = adj[g]
        adjoint[g] = adj[g].astype(bf16)

    for g in every:
        back[g] = lax.dot_general(
            adjoint[g], predict[g, 0], nt, preferred_element_type=f32
        ).astype(bf16)

    def pack(dst, peer):
        for k in range(cap):
            dst[k * chans : (k + 1) * chans] = back[held_ref[0, peer * cap + k]]

    def give(peer, mine):
        return to_block(ret_send.at[peer], ret_recv.at[mine], ret_ss.at[peer], ret_rs.at[mine], peer)

    def give_back(peer):
        pack(ret_send.at[peer], peer)
        give(peer, me).start()

    each_peer(give_back)
    pack(ret_recv.at[me], me)

    @pl.when(has_prev)
    def _():
        for g in range(nbd):
            seam_ret[g] = lax.dot_general(
                adjoint[g], predict[g, 1], nt, preferred_element_type=f32
            ).astype(bf16)
        seam_bwd.start()

    each_peer(lambda peer: share(me, peer).wait_recv(), nearest=True)
    line = sq_recv[0]
    for d in range(1, nblock):
        line = line + sq_recv[d]
    rg_send[...] = line

    def share_region(peer, mine):
        return to_region(rg_send, rg_recv.at[mine], rg_ss.at[peer], rg_rs.at[mine], peer)

    each_region(lambda peer: share_region(peer, region).start())
    rg_recv[region] = line

    @pl.when(has_next)
    def _():
        seam_where_in = to_region(seam_tgt, seam_tgt_in, seam_ss.at[1], seam_rs.at[1], up)
        seam_where_in.wait_recv()
        mask = jnp.where(
            seam_tgt_in[...] == lax.broadcasted_iota(i32, (rows, rows), 0), 1.0, 0.0
        ).astype(bf16)
        seam_bwd.wait_recv()
        got = jnp.dot(mask, seam_ret_in[...].reshape(rows, width), preferred_element_type=f32)
        out_ref[...] = out_ref[...] - got.reshape(nbd, chans, width)

    def add(pair):
        blocks_back = ret_recv[pl.ds(pair * group, group)].reshape(group * part, width)
        got = jnp.dot(spread[pair], blocks_back, preferred_element_type=f32)
        out_ref[...] = out_ref[...] - got.reshape(nbd, chans, width)

    each_peer(lambda peer: give(me, peer).wait_recv(), nearest=True)
    for pair in range(nblock // group):
        add(pair)

    each_region(lambda peer: share_region(region, peer).wait_recv())
    total = rg_recv[0]
    for r in range(1, nregion):
        total = total + rg_recv[r]
    total_live = jnp.sum(jnp.where(live_lane, total, 0.0), axis=1, keepdims=True)
    blocks = nbd * nblock * nregion
    gtau_ref[...] = (
        0.5 * total[:, :chans] - 0.5 * width * total_live / tau_ref[...]
    ) / (blocks * width)

    def sent(peer):
        request(peer, me).wait_send()
        unless_far(peer, lambda: serve(peer, me).wait_send())
        give(peer, me).wait_send()
        share(peer, me).wait_send()

    each_peer(sent)
    if ends:

        @pl.when(at_end)
        def _():
            far_copy.wait_send()
            relay.wait_send()

    each_region(lambda peer: share_region(peer, region).wait_send())

    @pl.when(has_next)
    def _():
        seam_fwd.wait_send()

    @pl.when(has_prev)
    def _():
        seam_where.wait_send()
        seam_bwd.wait_send()


def shards(obs, predict, factor, tau, nbr_dev, nbr_slot, counts):
    nbd, chans, width = obs.shape
    nblock = lax.axis_size("block")
    nregion = lax.axis_size("region")
    cap = max(2, 2 * nbd // nblock)
    rows = nbd * chans
    part = cap * chans
    lanes = -(-part // LANES) * LANES
    group = 2 if nblock % 2 == 0 and part % LANES == 0 else 1
    bf16, f32, i32 = jnp.bfloat16, jnp.float32, jnp.int32
    vmem = pl.BlockSpec(memory_space=pltpu.VMEM)
    hbm = pl.BlockSpec(memory_space=pltpu.HBM)
    dma = pltpu.SemaphoreType.DMA
    grad_obs, grad_tau = pl.pallas_call(
        functools.partial(kernel, nblock, nregion, cap),
        out_shape=(
            jax.ShapeDtypeStruct((nbd, chans, width), f32),
            jax.ShapeDtypeStruct((1, chans), f32),
        ),
        in_specs=[hbm] * 7,
        out_specs=(vmem, vmem),
        scratch_shapes=[
            pltpu.SMEM((1, nbd), i32),
            pltpu.SMEM((2, nbd), i32),
            pltpu.SMEM((1,), i32),
            pltpu.VMEM((1, chans), f32),
            pltpu.VMEM((nbd, chans, width), bf16),
            pltpu.VMEM((nbd, 2, width, width), bf16),
            pltpu.VMEM((nbd, width, width), bf16),
            pltpu.VMEM((nblock, 1, lanes), i32),
            pltpu.VMEM((nblock, 1, lanes), i32),
            pltpu.VMEM((nblock * cap, chans, width), bf16),
            pltpu.VMEM((nblock * cap + 2 * nbd, chans, width), bf16),
            pltpu.VMEM((nblock, part, width), bf16),
            pltpu.VMEM((nblock, part, width), bf16),
            pltpu.VMEM((nbd, chans, width), bf16),
            pltpu.VMEM((1, rows), i32),
            pltpu.VMEM((1, rows), i32),
            pltpu.VMEM((nbd, chans, width), bf16),
            pltpu.VMEM((nbd, chans, width), bf16),
            pltpu.VMEM((1, LANES), i32),
            pltpu.SMEM((1, LANES), i32),
            pltpu.VMEM((nblock // group, rows, group * part), bf16),
            pltpu.VMEM((nbd, chans, width), f32),
            pltpu.VMEM((nbd + 1, chans, width), bf16),
            pltpu.VMEM((nbd, chans, width), bf16),
            pltpu.VMEM((1, LANES), f32),
            pltpu.VMEM((nblock, 1, LANES), f32),
            pltpu.VMEM((1, LANES), f32),
            pltpu.VMEM((nregion, 1, LANES), f32),
            dma((8,)),
            dma((nblock,)),
            dma((nblock,)),
            dma((nblock,)),
            dma((nblock,)),
            dma((nblock,)),
            dma((nblock,)),
            dma((nblock,)),
            dma((nblock,)),
            dma((nregion,)),
            dma((nregion,)),
            dma((3,)),
            dma((3,)),
            dma((2,)),
            dma((2,)),
        ],
        compiler_params=pltpu.CompilerParams(
            collective_id=0, has_side_effects=True, vmem_limit_bytes=48 << 20
        ),
        name="vecchia",
    )(
        *(
            value if value is counts else pltpu.with_memory_space_constraint(value, pltpu.HBM)
            for value in (nbr_dev.T, nbr_slot.T, counts, tau.reshape(1, chans), obs, predict, factor)
        )
    )
    return grad_obs, grad_tau.reshape(chans)


def solution(mesh):
    in_specs = (
        P(("region", "block"), None, None),
        P(("region", "block"), None, None, None),
        P(("region", "block"), None, None),
        P(),
        P(("region", "block"), None),
        P(("region", "block"), None),
        P(("region", "block")),
    )
    out_specs = (P(("region", "block"), None, None), P())
    return jax.shard_map(shards, mesh=mesh, in_specs=in_specs, out_specs=out_specs, check_vma=False)
```
